32 devices in a mesh: state: 8 (over z, y), member: 4 (over x, core).
Axes of the slice: x: 2, y: 2, z: 4, core: 2. Of those that a mesh axis runs over, the one named last changes fastest.
Arguments:
- anomalies: bfloat16 [64, 256, 1024], P('state', 'member'), may hold values from -6 to 6
- tapers: bfloat16 [2, 1024, 1024], replicated, may hold values from 0 to 1, as said below
- nbr_block: int32 [64, 12], P('state'), may hold values from 0 to 63, as said below
- taper_index: int32 [64, 12], P('state'), may hold values from 0 to 1
- pair_count: int32 [64], P('state'), may hold values from 5 to 12, as said below
- obs_cell: int32 [65536], P('state'), may hold values from 0 to 8191, as said below
- obs_value: float32 [65536], P('state'), may hold values from -3 to 3
Outputs:
- increments: float32 [64, 1024], P('state', 'member')
The draws below stay inside these ranges and needn't reach their ends.
Inputs may be any that keep to these rules, and one draw needn't show every extreme that they name: `nbr_block`: every slot of block i names a block whose state index (block // 8) lies within 2 of i // 8 around the closed loop of state indices; slot 0 names i itself, and slots 1 to 4 name blocks at state-index offsets -2 to 2 without 0, in rising order. Block i uses slots 0 to pair_count[i] - 1; at least one block uses all 12 slots. Observation r lies in variable obs_cell[r] of the 8192 variables held by state index r // 8192, counted block by block. `tapers`: Gaspari-Cohn taper values of pairs of variables.
All inputs are finite; a program needn't handle non-finite values.
Results may differ from the reference program's by a relative error of at most 0.0018.
Values may be sent and summed in bfloat16 or wider, within the bound.
A program may use at most 64 MiB of HBM per device.

```python
import jax
import jax.numpy as jnp
from jax import lax

B = 1024
M = 256
HOPS = 2
NEIGHBOUR_SLOTS = 12
KT = 2
BLK_DEV = 8
TOTAL_BLOCKS = 64
OBS_DEV = 8192
NOBS = 65536


def draw_tapers(key, part):
    place_key = jax.random.fold_in(key, 101)
    position = jax.random.uniform(place_key, (B, 2), dtype=jnp.float32)
    offset = 0.15 * jnp.arange(KT).astype(jnp.float32)[:, None, None]
    delta_x = position[None, :, None, 0] - position[None, None, :, 0] + offset
    delta_x = delta_x - jnp.floor(delta_x + 0.5)
    delta_y = position[None, :, None, 1] - position[None, None, :, 1] + 0.0 * offset
    delta_y = delta_y - jnp.floor(delta_y + 0.5)
    scaled = jnp.sqrt(delta_x * delta_x + delta_y * delta_y) / 0.06
    inner = -0.25 * scaled ** 5 + 0.5 * scaled ** 4 + 0.625 * scaled ** 3 - 5.0 / 3.0 * scaled ** 2 + 1.0
    safe = jnp.maximum(scaled, 1.0)
    outer = safe ** 5 / 12.0 - 0.5 * safe ** 4 + 0.625 * safe ** 3 + 5.0 / 3.0 * safe ** 2 - 5.0 * safe + 4.0 - 2.0 / (3.0 * safe)
    taper_value = jnp.where(scaled <= 1.0, inner, jnp.where(scaled <= 2.0, outer, 0.0))
    return jnp.clip(taper_value, 0.0, 1.0).astype(jnp.bfloat16)


def draw_nbr_block(key, part):
    block_numbers = jnp.arange(TOTAL_BLOCKS, dtype=jnp.int32)[:, None]
    home = block_numbers // BLK_DEV
    devices = TOTAL_BLOCKS // BLK_DEV
    fixed_offsets = jnp.concatenate([jnp.zeros((1,), jnp.int32), jnp.arange(-HOPS, 0, dtype=jnp.int32), jnp.arange(1, HOPS + 1, dtype=jnp.int32)])
    fixed_offsets = jnp.broadcast_to(fixed_offsets[None, :], (TOTAL_BLOCKS, 2 * HOPS + 1))
    random_offsets = jax.random.randint(jax.random.fold_in(key, 201), (TOTAL_BLOCKS, NEIGHBOUR_SLOTS - 2 * HOPS - 1), -HOPS, HOPS + 1, dtype=jnp.int32)
    offsets = jnp.concatenate([fixed_offsets, random_offsets], axis=1)
    within = jax.random.randint(jax.random.fold_in(key, 202), (TOTAL_BLOCKS, NEIGHBOUR_SLOTS), 0, BLK_DEV, dtype=jnp.int32)
    slot_ids = jnp.arange(NEIGHBOUR_SLOTS, dtype=jnp.int32)[None, :]
    within = jnp.where(slot_ids == 0, block_numbers % BLK_DEV, within)
    return (home + offsets + devices) % devices * BLK_DEV + within


def draw_pair_count(key, part):
    starting_count = jax.random.randint(jax.random.fold_in(key, 301), (TOTAL_BLOCKS,), 2 * HOPS + 1, 2 * HOPS + 5, dtype=jnp.int32)
    sudden_spike = jax.random.randint(jax.random.fold_in(key, 302), (TOTAL_BLOCKS,), 0, 8, dtype=jnp.int32) == 0
    enforced_flag = jax.random.randint(jax.random.fold_in(key, 303), (), 0, TOTAL_BLOCKS, dtype=jnp.int32)
    block_numbers = jnp.arange(TOTAL_BLOCKS, dtype=jnp.int32)
    return jnp.where(sudden_spike | (block_numbers == enforced_flag), NEIGHBOUR_SLOTS, starting_count).astype(jnp.int32)


def draw_obs_cell(key, part):
    return jax.random.randint(jax.random.fold_in(key, 401), (NOBS,), 0, BLK_DEV * B, dtype=jnp.int32)


def with_ends(array, rng, least, high):
    longest = array.shape.index(max(array.shape))
    spots = []
    for shift in (0, 1):
        where = [jax.random.randint(jax.random.fold_in(rng, axis), (), 0, length) for axis, length in enumerate(array.shape)]
        where[longest] = (where[longest] + shift) % array.shape[longest]
        spots.append(tuple(where))
    return array.at[spots[0]].set(least).at[spots[1]].set(high)


def levels(own_key, extent, split, least, top_value):
    loudness = 1.0
    for dim, blocks in split:
        steps = jax.random.uniform(jax.random.fold_in(jax.random.fold_in(own_key, 6), dim), (blocks,), jnp.float32, least / len(split), top_value / len(split))
        loudness = loudness * jnp.repeat(jnp.exp(steps), extent[dim] // blocks).reshape((-1,) + (1,) * (len(extent) - 1 - dim))
    return loudness


def normal_values(key, dims, width, bound, shards=(), kind=jnp.bfloat16):
    level = levels(key, dims, shards, -0.22, 0.18) if shards else 1.0
    array = jax.random.normal(key, dims, jnp.float32) * width * level
    return jnp.minimum(jnp.maximum(array, -bound), bound).astype(kind)


def setup_inputs(seed: int = 0) -> dict:
    arg_keys = jax.random.split(jax.random.key(seed), 8)
    anomalies = normal_values(arg_keys[0], (TOTAL_BLOCKS, M, B), 1.0, 6.0, ((0, 8), (1, 4)))
    tapers = draw_tapers(jax.random.fold_in(arg_keys[7], 71), 0)
    nbr_block = draw_nbr_block(jax.random.fold_in(arg_keys[7], 71), 0)
    taper_index = with_ends(jax.random.randint(arg_keys[3], (TOTAL_BLOCKS, NEIGHBOUR_SLOTS), 0, KT), jax.random.fold_in(arg_keys[3], 1), 0, KT - 1).astype(jnp.int32)
    pair_count = draw_pair_count(jax.random.fold_in(arg_keys[7], 71), 0)
    obs_cell = draw_obs_cell(jax.random.fold_in(arg_keys[7], 71), 0)
    obs_value = normal_values(arg_keys[6], (NOBS,), 0.5, 3.0, ((0, 8),), jnp.float32)
    return {"anomalies": anomalies, "tapers": tapers, "nbr_block": nbr_block, "taper_index": taper_index, "pair_count": pair_count, "obs_cell": obs_cell, "obs_value": obs_value}


def reference(anomalies, tapers, nbr_block, taper_index, pair_count, obs_cell, obs_value):
    row_ids = jnp.arange(NOBS, dtype=jnp.int32)
    global_cells = (row_ids // OBS_DEV) * (BLK_DEV * B) + obs_cell.astype(jnp.int32)
    observation_residual = jnp.zeros((TOTAL_BLOCKS * B,), jnp.float32).at[global_cells].add(obs_value).reshape(TOTAL_BLOCKS, B)
    weighted_low = (anomalies.astype(jnp.float32) * observation_residual[:, None, :]).astype(jnp.bfloat16)
    weighted_low = lax.optimization_barrier(weighted_low)
    slot_ids = jnp.arange(NEIGHBOUR_SLOTS, dtype=jnp.int32)
    tile_ids = jnp.arange(KT, dtype=jnp.int32)
    taper_wide = tapers.astype(jnp.float32)

    def one_block(block_id):
        is_valid = slot_ids < pair_count[block_id]
        selector = (is_valid[:, None] & (taper_index[block_id][:, None] == tile_ids[None, :])).astype(jnp.float32)
        panels = weighted_low[nbr_block[block_id]].astype(jnp.float32)
        gathered_groups = jnp.einsum('st,smb->tmb', selector, panels,
                             precision=lax.Precision.HIGHEST).astype(jnp.bfloat16)
        gathered_groups = lax.optimization_barrier(gathered_groups).astype(jnp.float32)
        running = jnp.zeros((M, B), jnp.float32)
        for tile_id in range(KT):
            running = running + jnp.dot(gathered_groups[tile_id], taper_wide[tile_id].T,
                                        precision=lax.Precision.HIGHEST)
        member_terms = anomalies[block_id].astype(jnp.float32) * running
        return jnp.sum(member_terms, axis=0) / jnp.float32(M - 1)

    return lax.map(one_block, jnp.arange(TOTAL_BLOCKS, dtype=jnp.int32))
```

```python
import functools

import jax
import jax.numpy as jnp
from jax import lax
from jax.experimental import pallas as pl
from jax.experimental.pallas import tpu as pltpu
from jax.sharding import PartitionSpec as P

M = 256
HOPS = 2
KT = 2
LANES = 128
MC = 16
PIECES = 2
MESH = pl.DeviceIdType.MESH


def kernel(
    states, members, slots,
    tab0, tabs, cells, values, anom, tapers, out,
    av, tv, r1, r2, tab_in, idx, innov, innov_in, hot, low, z, own_w, wr, acc, part, got,
    tab_s, tab_r, idx_s, av_s, tv_s, s1, q1, s2, q2, in_s, in_r, ps, pr,
):
    blocks, mem, width = anom.shape
    chunks = mem // MC
    half = blocks // PIECES
    groups = width // LANES
    cols = width // members
    zero_panel = KT * 3 * blocks
    d = lax.axis_index("state")
    me = lax.axis_index("member")
    even = d % 2 == 0

    def at(ds, dm):
        return ((d + ds + states) % states, (me + dm) % members)

    barrier = pltpu.get_barrier_semaphore()
    count = 0
    for ds in range(-HOPS, HOPS + 1):
        for dm in range(members):
            if ds or dm:
                pl.semaphore_signal(barrier, inc=1, device_id=at(ds, dm), device_id_type=MESH)
                count += 1

    load_a = pltpu.make_async_copy(anom, av, av_s)
    load_t = pltpu.make_async_copy(tapers, tv, tv_s)
    load_a.start()
    load_t.start()
    pl.semaphore_wait(barrier, count)

    def remote(src, dst, send, recv, target):
        return pltpu.make_async_remote_copy(
            src_ref=src, dst_ref=dst, send_sem=send, recv_sem=recv,
            device_id=target, device_id_type=MESH,
        )

    def piece(ref, c, h):
        return ref.at[pl.ds(h * half, half), pl.ds(pl.multiple_of(c * MC, MC), MC), :]

    def send2(c, h):
        return remote(piece(anom, c, h), piece(r2, c, h), s2.at[c, h], q2.at[c, h], at(2, 0))

    def send1(c, h):
        return remote(piece(anom, c, h), piece(r1, c, h), s1.at[c, h], q1.at[c, h], at(1, 0))

    def relay(c, h):
        return remote(piece(r2, c, h), piece(r1, c, h), s1.at[c, h], q1.at[c, h], at(-1, 0))

    def send_tab(u):
        return remote(tabs.at[u - 1], tab_in.at[u - 1], tab_s.at[u - 1], tab_r.at[u - 1], at(u, 0))

    def send_innov(u):
        return remote(innov, innov_in.at[u - 1], in_s.at[u - 1], in_r.at[u - 1], at(u, 0))

    def send_part(u, k):
        return remote(
            part.at[u, (me + k) % members], got.at[u, k], ps.at[u, k], pr.at[u, k], at(-u, k)
        )

    for u in (1, 2):
        send_tab(u).start()
    for h in range(PIECES):
        send2(0, h).start()

    @pl.when(even)
    def _():
        for h in range(PIECES):
            send1(0, h).start()

    acc[...] = jnp.zeros_like(acc)

    def hot_row(k, carry):
        cell = cells[pl.ds(k, 1), :]
        value = values[pl.ds(k, 1), :]
        lo = cell & (LANES - 1)
        block = cell // width
        group = (cell // LANES) % groups
        hi = group * blocks + block
        v1 = value.astype(jnp.bfloat16).astype(jnp.float32)
        rest = value - v1
        v2 = rest.astype(jnp.bfloat16).astype(jnp.float32)
        v3 = rest - v2
        rows = blocks * groups
        same = lax.broadcasted_iota(jnp.int32, (rows, LANES), 0) == hi
        where = pl.ds(pl.multiple_of(k * LANES, LANES), LANES)
        for n, v in enumerate((v1, v2, v3)):
            hot[pl.ds(n * rows, rows), where] = jnp.where(
                same, jnp.broadcast_to(v, (rows, LANES)), 0.0
            ).astype(jnp.bfloat16)
        low[:, where] = jnp.where(
            lax.broadcasted_iota(jnp.int32, (LANES, LANES), 0) == lo, 1.0, 0.0
        ).astype(jnp.bfloat16)
        return carry

    lax.fori_loop(0, cells.shape[0], hot_row, 0)
    rows = blocks * groups
    sums = lax.dot_general(
        hot[...], low[...], (((1,), (1,)), ((), ())), preferred_element_type=jnp.float32
    )
    total = sums[0:rows] + sums[rows : 2 * rows] + sums[2 * rows : 3 * rows]
    for g in range(groups):
        innov[:, g * LANES : (g + 1) * LANES] = total[g * blocks : (g + 1) * blocks]
    for u in (1, 2):
        send_innov(u).start()

    def rest_of(c, carry):
        for h in range(PIECES):
            send2(c, h).start()

        @pl.when(even)
        def _():
            for h in range(PIECES):
                send1(c, h).start()

        return carry

    lax.fori_loop(1, chunks, rest_of, 0)

    load_a.wait()
    for j in range(blocks):
        own_w[:, j] = (
            av[j].astype(jnp.float32) * innov[pl.ds(j, 1), :]
        ).astype(jnp.bfloat16).reshape(chunks, MC, width)
    load_t.wait()
    nw = width // 2

    def own_z(n, carry):
        c, t, x = n // (2 * KT), (n // 2) % KT, n % 2
        where = pl.ds(pl.multiple_of(x * nw, nw), nw)
        res = lax.dot_general(
            own_w[c].reshape(blocks * MC, width), tv[t, where, :],
            (((1,), (1,)), ((), ())), preferred_element_type=jnp.float32,
        )
        z[c, pl.ds(t * 3 * blocks, blocks), :, where] = res.reshape(blocks, MC, nw)
        return carry

    lax.fori_loop(0, chunks * KT * 2, own_z, 0)
    for c in range(chunks):
        z[c, zero_panel] = jnp.zeros((MC, width), jnp.float32)

    for u in (1, 2):
        send_tab(u).wait_recv()
        fill = pltpu.make_async_copy(tab_in.at[u - 1], idx.at[u - 1], idx_s.at[u - 1])
        fill.start()
        fill.wait()

    def pairs(c, u, table, source):
        def one(i, carry):
            total = z[c, table(i, 0)]
            for s in range(1, slots):
                total = total + z[c, table(i, s)]
            value = source[i, pl.ds(pl.multiple_of(c * MC, MC), MC), :].astype(jnp.float32) * total
            acc[u, i] += jnp.sum(value.reshape(MC // 8, 8, width), axis=0)
            return carry

        lax.fori_loop(0, blocks, one, 0)

    def fold(u):
        for i in range(blocks):
            row = jnp.sum(acc[u, i], axis=0, keepdims=True)
            for m in range(members):
                part[u, m, i : i + 1, :] = row[:, m * cols : (m + 1) * cols]

    def step(c, carry):
        for h in range(PIECES):
            send2(c, h).wait_recv()

            @pl.when(jnp.logical_not(even))
            def _():
                relay(c, h).start()

        pairs(c, 2, lambda i, s: idx[1, i, s], r2)
        for h in range(PIECES):
            send1(c, h).wait_recv()
        pairs(c, 1, lambda i, s: idx[0, i, s], r1)

        @pl.when(c == 0)
        def _():
            for u in (1, 2):
                send_innov(u).wait_recv()

        @pl.when(c == chunks - 1)
        def _():
            for u in (2, 1):
                fold(u)
                for k in range(members):
                    send_part(u, k).start()

        for g, r in enumerate((r1, r2)):
            for j in range(blocks):
                wr[g * blocks + j] = (
                    r[j, pl.ds(pl.multiple_of(c * MC, MC), MC), :].astype(jnp.float32)
                    * innov_in[g, pl.ds(j, 1), :]
                ).astype(jnp.bfloat16)

        def far_z(n, carry):
            t, x = n // 2, n % 2
            where = pl.ds(pl.multiple_of(x * nw, nw), nw)
            res = lax.dot_general(
                wr[...].reshape(2 * blocks * MC, width), tv[t, where, :],
                (((1,), (1,)), ((), ())), preferred_element_type=jnp.float32,
            )
            z[c, pl.ds(t * 3 * blocks + blocks, 2 * blocks), :, where] = res.reshape(
                2 * blocks, MC, nw
            )
            return carry

        lax.fori_loop(0, KT * 2, far_z, 0)
        pairs(c, 0, lambda i, s: tab0[i, s], av)
        return carry

    lax.fori_loop(0, chunks, step, 0)
    fold(0)
    for k in range(1, members):
        send_part(0, k).start()
    total = part[0, me]
    for u in (2, 1, 0):
        for k in range(members):
            if u or k:
                send_part(u, k).wait_recv()
                total = total + got[u, k]
    out[...] = total / jnp.float32(M - 1)

    for u in (0, 1, 2):
        for k in range(members):
            if u or k:
                send_part(u, k).wait_send()
    for u in (1, 2):
        send_tab(u).wait_send()
        send_innov(u).wait_send()

    def drain(c, carry):
        for h in range(PIECES):
            send2(c, h).wait_send()
            send1(c, h).wait_send()
        return carry

    lax.fori_loop(0, chunks, drain, 0)


def on_device(states, members, anomalies, tapers, nbr_block, taper_index, pair_count, obs_cell, obs_value):
    blocks, mem, width = anomalies.shape
    slots = nbr_block.shape[1]
    chunks = mem // MC
    cols = width // members
    d = lax.axis_index("state")
    gap = (nbr_block // blocks - d + HOPS + states) % states - HOPS
    valid = jnp.arange(slots, dtype=jnp.int32)[None, :] < pair_count[:, None]
    base = taper_index * (3 * blocks) + nbr_block % blocks
    none = KT * 3 * blocks
    tab0 = jnp.where(valid & (gap <= 0), base - gap * blocks, none)
    tabs = jnp.stack([jnp.where(valid & (gap == u), base, none) for u in (1, 2)])
    tabs = jnp.pad(tabs, ((0, 0), (0, 0), (0, LANES - slots)))
    cells = obs_cell.reshape(-1, LANES)
    values = obs_value.reshape(-1, LANES)
    rows = blocks * (width // LANES)
    dma = pltpu.SemaphoreType.DMA
    any_space = pl.BlockSpec(memory_space=pl.ANY)
    vmem = pl.BlockSpec(memory_space=pltpu.VMEM)
    return pl.pallas_call(
        functools.partial(kernel, states, members, slots),
        out_shape=jax.ShapeDtypeStruct((blocks, cols), jnp.float32),
        in_specs=[pl.BlockSpec(memory_space=pltpu.SMEM), any_space, vmem, vmem, any_space, any_space],
        out_specs=vmem,
        scratch_shapes=[
            pltpu.VMEM((blocks, mem, width), jnp.bfloat16),
            pltpu.VMEM(tapers.shape, jnp.bfloat16),
            pltpu.VMEM((blocks, mem, width), jnp.bfloat16),
            pltpu.VMEM((blocks, mem, width), jnp.bfloat16),
            pltpu.VMEM((2, blocks, LANES), jnp.int32),
            pltpu.SMEM((2, blocks, LANES), jnp.int32),
            pltpu.VMEM((blocks, width), jnp.float32),
            pltpu.VMEM((2, blocks, width), jnp.float32),
            pltpu.VMEM((3 * rows, obs_cell.shape[0]), jnp.bfloat16),
            pltpu.VMEM((LANES, obs_cell.shape[0]), jnp.bfloat16),
            pltpu.VMEM((chunks, KT * 3 * blocks + 1, MC, width), jnp.float32),
            pltpu.VMEM((chunks, blocks, MC, width), jnp.bfloat16),
            pltpu.VMEM((2 * blocks, MC, width), jnp.bfloat16),
            pltpu.VMEM((3, blocks, 8, width), jnp.float32),
            pltpu.VMEM((3, members, blocks, cols), jnp.float32),
            pltpu.VMEM((3, members, blocks, cols), jnp.float32),
            dma((2,)), dma((2,)), dma((2,)), dma, dma,
            dma((chunks, PIECES)), dma((chunks, PIECES)),
            dma((chunks, PIECES)), dma((chunks, PIECES)),
            dma((2,)), dma((2,)),
            dma((3, members)), dma((3, members)),
        ],
        compiler_params=pltpu.CompilerParams(
            collective_id=0, has_side_effects=True, vmem_limit_bytes=48 * 1024 * 1024
        ),
    )(tab0, tabs, cells, values, anomalies, tapers)


def solution(mesh):
    placed = (
        P("state", "member", None),
        P(),
        P("state", None),
        P("state", None),
        P("state"),
        P("state"),
        P("state"),
    )
    return jax.shard_map(
        functools.partial(on_device, mesh.shape["state"], mesh.shape["member"]),
        mesh=mesh, in_specs=placed, out_specs=P("state", "member"), check_vma=False,
    )
```

```python
import functools

import jax
import jax.numpy as jnp
from jax import lax
from jax.experimental import pallas as pl
from jax.experimental.pallas import tpu as pltpu
from jax.sharding import PartitionSpec as P

M = 256
HOPS = 2
KT = 2
LANES = 128
MC = 16
PIECES = 1
MESH = pl.DeviceIdType.MESH


def kernel(
    states, members, slots,
    tab0_hbm, tabs, cells_hbm, values_hbm, anom, tapers, out,
    tab0, cells, values, obs_s, av, tv, r1, r2, tab_in, idx, innov, innov_in, hot, low, z, own_w, wr, acc, part, got,
    tab_s, tab_r, idx_s, av_s, tv_s, s1, q1, s2, q2, in_s, in_r, ps, pr, peers,
):
    blocks, mem, width = anom.shape
    chunks = mem // MC
    half = blocks // PIECES
    groups = width // LANES
    cols = width // members
    zero_panel = KT * 3 * blocks
    d = lax.axis_index("state")
    me = lax.axis_index("member")
    odd = d % 2
    sign = 1 - 2 * odd
    heavy = chunks // 2

    def at(ds, dm):
        return ((d + ds + states) % states, (me + dm) % members)

    barrier = pltpu.get_barrier_semaphore()
    greeted = [(sign, 0), (2, 0), (-2, 0)] + [(0, k) for k in range(1, members)]
    for ds, dm in greeted:
        pl.semaphore_signal(barrier, inc=1, device_id=at(ds, dm), device_id_type=MESH)

    load_a = pltpu.make_async_copy(anom, av, av_s)
    load_t = pltpu.make_async_copy(tapers, tv, tv_s)
    load_c = pltpu.make_async_copy(cells_hbm, cells, obs_s.at[0])
    load_v = pltpu.make_async_copy(values_hbm, values, obs_s.at[1])
    load_i = pltpu.make_async_copy(tab0_hbm, tab0, obs_s.at[2])
    for load in (load_c, load_v, load_i, load_a, load_t):
        load.start()

    def remote(src, dst, send, recv, target):
        return pltpu.make_async_remote_copy(
            src_ref=src, dst_ref=dst, send_sem=send, recv_sem=recv,
            device_id=target, device_id_type=MESH,
        )

    def members_of(c, shift):
        return pl.ds(pl.multiple_of(((c + shift * heavy) % chunks) * MC, MC), MC)

    def piece(ref, c, h, shift):
        return ref.at[pl.ds(h * half, half), members_of(c, shift), :]

    def send2(c, h):
        return remote(
            piece(anom, c, h, odd), piece(r2, c, h, 0), s2.at[c, h], q2.at[c, h], at(-2 * sign, 0)
        )

    def send1(c):
        return remote(
            anom.at[:, members_of(c, 1 - odd), :], r1.at[:, members_of(c, 0), :],
            s1.at[c], q1.at[c], at(sign, 0),
        )

    def to(u):
        return sign if u == 1 else -2 * sign

    def send_tab(u):
        return remote(tabs.at[u - 1], tab_in.at[u - 1], tab_s.at[u - 1], tab_r.at[u - 1], at(to(u), 0))

    def send_innov(u):
        return remote(innov, innov_in.at[u - 1], in_s.at[u - 1], in_r.at[u - 1], at(to(u), 0))

    def send_part(u, k):
        return remote(
            part.at[u, (me + k) % members], got.at[u, k], ps.at[u, k], pr.at[u, k],
            at((0, sign, 2 * sign)[u], k),
        )

    acc[...] = jnp.zeros_like(acc)

    def hot_row(k, carry):
        cell = cells[pl.ds(k, 1), :]
        value = values[pl.ds(k, 1), :]
        lo = cell & (LANES - 1)
        block = cell // width
        group = (cell // LANES) % groups
        hi = group * blocks + block
        v1 = value.astype(jnp.bfloat16).astype(jnp.float32)
        rest = value - v1
        v2 = rest.astype(jnp.bfloat16).astype(jnp.float32)
        v3 = rest - v2
        rows = blocks * groups
        same = lax.broadcasted_iota(jnp.int32, (rows, LANES), 0) == hi
        where = pl.ds(pl.multiple_of(k * LANES, LANES), LANES)
        for n, v in enumerate((v1, v2, v3)):
            hot[pl.ds(n * rows, rows), where] = jnp.where(
                same, jnp.broadcast_to(v, (rows, LANES)), 0.0
            ).astype(jnp.bfloat16)
        low[:, where] = jnp.where(
            lax.broadcasted_iota(jnp.int32, (LANES, LANES), 0) == lo, 1.0, 0.0
        ).astype(jnp.bfloat16)
        return carry

    load_c.wait()
    load_v.wait()
    load_i.wait()
    lax.fori_loop(0, cells.shape[0], hot_row, 0)
    rows = blocks * groups
    sums = lax.dot_general(
        hot[...], low[...], (((1,), (1,)), ((), ())), preferred_element_type=jnp.float32
    )
    total = sums[0:rows] + sums[rows : 2 * rows] + sums[2 * rows : 3 * rows]
    for g in range(groups):
        innov[:, g * LANES : (g + 1) * LANES] = total[g * blocks : (g + 1) * blocks]
    pl.semaphore_wait(barrier, len(greeted))
    for u in (1, 2):
        send_tab(u).start()
        send_innov(u).start()

    def send_all(c, carry):
        for h in range(PIECES):
            send2(c, h).start()
        return carry

    for c in range(heavy):
        send1(c).start()
    lax.fori_loop(0, chunks, send_all, 0)
    for k in range(1, members):
        pl.semaphore_signal(peers, inc=1, device_id=at(0, k), device_id_type=MESH)

    load_a.wait()
    for c in range(chunks):
        for j in range(blocks):
            own_w[c, j] = (
                av[j, members_of(c, odd), :].astype(jnp.float32) * innov[pl.ds(j, 1), :]
            ).astype(jnp.bfloat16)
    load_t.wait()
    nw = width // 4

    def own_z(n, carry):
        t, x = n // 4, n % 4
        where = pl.ds(pl.multiple_of(x * nw, nw), nw)
        res = lax.dot_general(
            own_w[...].reshape(chunks * blocks * MC, width), tv[t, where, :],
            (((1,), (1,)), ((), ())), preferred_element_type=jnp.float32,
        )
        z[:, pl.ds(t * 3 * blocks, blocks), :, where] = res.reshape(chunks, blocks, MC, nw)
        return carry

    lax.fori_loop(0, KT * 4, own_z, 0)
    for c in range(heavy, chunks):
        for t in range(KT):
            z[c, (t * 3 + 1) * blocks : (t * 3 + 2) * blocks] = jnp.zeros((blocks, MC, width), jnp.float32)
    for c in range(chunks):
        z[c, zero_panel] = jnp.zeros((MC, width), jnp.float32)

    for u in (1, 2):
        send_tab(u).wait_recv()
        fill = pltpu.make_async_copy(tab_in.at[u - 1], idx.at[u - 1], idx_s.at[u - 1])
        fill.start()
        fill.wait()

    def pairs(c, u, table, source, shift):
        def one(i, carry):
            total = z[c, table(i, 0)]
            for s in range(1, slots):
                total = total + z[c, table(i, s)]
            value = source[i, members_of(c, shift), :].astype(jnp.float32) * total
            acc[u, i] += jnp.sum(value.reshape(MC // 8, 8, width), axis=0)
            return carry

        lax.fori_loop(0, blocks, one, 0)

    def fold(u):
        for i in range(blocks):
            row = jnp.sum(acc[u, i], axis=0, keepdims=True)
            for m in range(members):
                part[u, m, i : i + 1, :] = row[:, m * cols : (m + 1) * cols]

    def step(full, c, carry):
        for h in range(PIECES):
            send2(c, h).wait_recv()
        if full:
            send1(c).wait_recv()
        else:
            pairs(c, 2, lambda i, s: idx[1, i, s], r2, 0)

            @pl.when(c == chunks - 1)
            def _():
                fold(2)
                for k in range(members):
                    send_part(2, k).start()

        first = 0 if full else blocks
        for g, r in enumerate((r1, r2)):
            if g or full:
                for j in range(blocks):
                    wr[g * blocks + j] = (
                        r[j, members_of(c, 0), :].astype(jnp.float32)
                        * innov_in[g, pl.ds(j, 1), :]
                    ).astype(jnp.bfloat16)
        count = 2 * blocks - first

        def far_z(n, carry):
            t, x = n // 4, n % 4
            where = pl.ds(pl.multiple_of(x * nw, nw), nw)
            res = lax.dot_general(
                wr[pl.ds(first, count)].reshape(count * MC, width), tv[t, where, :],
                (((1,), (1,)), ((), ())), preferred_element_type=jnp.float32,
            )
            z[c, pl.ds(t * 3 * blocks + blocks + first, count), :, where] = res.reshape(
                count, MC, nw
            )
            return carry

        lax.fori_loop(0, KT * 4, far_z, 0)
        if full:
            pairs(c, 2, lambda i, s: idx[1, i, s], r2, 0)
            pairs(c, 1, lambda i, s: idx[0, i, s], r1, 0)
        pairs(c, 0, lambda i, s: tab0[i, s], av, odd)
        return carry

    for u in (1, 2):
        send_innov(u).wait_recv()
    lax.fori_loop(0, heavy, functools.partial(step, True), 0)
    fold(1)
    pl.semaphore_wait(peers, members - 1)
    for k in range(members):
        send_part(1, k).start()
    lax.fori_loop(heavy, chunks, functools.partial(step, False), 0)
    fold(0)
    for k in range(1, members):
        send_part(0, k).start()
    total = part[0, me]
    for u in (2, 1, 0):
        for k in range(members):
            if u or k:
                send_part(u, k).wait_recv()
                total = total + got[u, k]
    out[...] = total / jnp.float32(M - 1)

    for u in (0, 1, 2):
        for k in range(members):
            if u or k:
                send_part(u, k).wait_send()
    for u in (1, 2):
        send_tab(u).wait_send()
        send_innov(u).wait_send()

    def drain(c, carry):
        for h in range(PIECES):
            send2(c, h).wait_send()
        return carry

    lax.fori_loop(0, chunks, drain, 0)
    for c in range(heavy):
        send1(c).wait_send()


def on_device(states, members, anomalies, tapers, nbr_block, taper_index, pair_count, obs_cell, obs_value):
    blocks, mem, width = anomalies.shape
    slots = nbr_block.shape[1]
    chunks = mem // MC
    cols = width // members
    d = lax.axis_index("state")
    gap = (nbr_block // blocks - d + HOPS + states) % states - HOPS
    valid = jnp.arange(slots, dtype=jnp.int32)[None, :] < pair_count[:, None]
    base = taper_index * (3 * blocks) + nbr_block % blocks
    none = KT * 3 * blocks
    sign = 1 - 2 * (d % 2)
    gap = gap * sign
    tab0 = jnp.where(valid & (gap >= 0), base + gap * blocks, none)
    tab0 = jnp.pad(tab0, ((0, 0), (0, LANES - slots)))
    near = jnp.where(gap == 1, base, jnp.where(gap == -1, base + 2 * blocks, none))
    far = jnp.where(gap == -2, base, jnp.where(gap == -1, base + blocks, none))
    tabs = jnp.where(valid, jnp.stack([near, far]), none)
    tabs = jnp.pad(tabs, ((0, 0), (0, 0), (0, LANES - slots)))
    cells = obs_cell.reshape(-1, LANES)
    values = obs_value.reshape(-1, LANES)
    rows = blocks * (width // LANES)
    dma = pltpu.SemaphoreType.DMA
    any_space = pl.BlockSpec(memory_space=pl.ANY)
    vmem = pl.BlockSpec(memory_space=pltpu.VMEM)
    return pl.pallas_call(
        functools.partial(kernel, states, members, slots),
        out_shape=jax.ShapeDtypeStruct((blocks, cols), jnp.float32),
        in_specs=[any_space] * 6,
        out_specs=vmem,
        scratch_shapes=[
            pltpu.SMEM((blocks, LANES), jnp.int32),
            pltpu.VMEM(cells.shape, jnp.int32),
            pltpu.VMEM(values.shape, jnp.float32),
            dma((3,)),
            pltpu.VMEM((blocks, mem, width), jnp.bfloat16),
            pltpu.VMEM(tapers.shape, jnp.bfloat16),
            pltpu.VMEM((blocks, mem, width), jnp.bfloat16),
            pltpu.VMEM((blocks, mem, width), jnp.bfloat16),
            pltpu.VMEM((2, blocks, LANES), jnp.int32),
            pltpu.SMEM((2, blocks, LANES), jnp.int32),
            pltpu.VMEM((blocks, width), jnp.float32),
            pltpu.VMEM((2, blocks, width), jnp.float32),
            pltpu.VMEM((3 * rows, obs_cell.shape[0]), jnp.bfloat16),
            pltpu.VMEM((LANES, obs_cell.shape[0]), jnp.bfloat16),
            pltpu.VMEM((chunks, KT * 3 * blocks + 1, MC, width), jnp.float32),
            pltpu.VMEM((chunks, blocks, MC, width), jnp.bfloat16),
            pltpu.VMEM((2 * blocks, MC, width), jnp.bfloat16),
            pltpu.VMEM((3, blocks, 8, width), jnp.float32),
            pltpu.VMEM((3, members, blocks, cols), jnp.float32),
            pltpu.VMEM((3, members, blocks, cols), jnp.float32),
            dma((2,)), dma((2,)), dma((2,)), dma, dma,
            dma((chunks,)), dma((chunks,)),
            dma((chunks, PIECES)), dma((chunks, PIECES)),
            dma((2,)), dma((2,)),
            dma((3, members)), dma((3, members)),
            pltpu.SemaphoreType.REGULAR,
        ],
        compiler_params=pltpu.CompilerParams(
            collective_id=0, has_side_effects=True, vmem_limit_bytes=67_043_328
        ),
    )(tab0, tabs, cells, values, anomalies, tapers)


def solution(mesh):
    placed = (
        P("state", "member", None),
        P(),
        P("state", None),
        P("state", None),
        P("state"),
        P("state"),
        P("state"),
    )
    return jax.shard_map(
        functools.partial(on_device, mesh.shape["state"], mesh.shape["member"]),
        mesh=mesh, in_specs=placed, out_specs=P("state", "member"), check_vma=False,
    )
```

```python
import functools

import jax
import jax.numpy as jnp
from jax import lax
from jax.experimental import pallas as pl
from jax.experimental.pallas import tpu as pltpu
from jax.sharding import PartitionSpec as P

M = 256
HOPS = 2
KT = 2
LANES = 128
MC = 16
PIECES = 1
MESH = pl.DeviceIdType.MESH


def kernel(
    states, members, slots,
    tab0_hbm, tabs, cells_hbm, values_hbm, anom, tapers, out,
    tab0, cells, values, obs_s, av, tv, r1, r2, tab_in, idx, innov, innov_in, hot, low, z, own_w, wr, acc, part, got,
    tab_s, tab_r, idx_s, av_s, tv_s, s1, q1, s2, q2, in_s, in_r, ps, pr, peers,
):
    blocks, mem, width = anom.shape
    chunks = mem // MC
    half = blocks // PIECES
    groups = width // LANES
    cols = width // members
    zero_panel = KT * 3 * blocks
    d = lax.axis_index("state")
    me = lax.axis_index("member")
    odd = d % 2
    sign = 1 - 2 * odd
    heavy = chunks // 2

    def at(ds, dm):
        return ((d + ds + states) % states, (me + dm) % members)

    barrier = pltpu.get_barrier_semaphore()
    greeted = [(sign, 0), (2, 0), (-2, 0)] + [(0, k) for k in range(1, members)]
    for ds, dm in greeted:
        pl.semaphore_signal(barrier, inc=1, device_id=at(ds, dm), device_id_type=MESH)

    load_a = pltpu.make_async_copy(anom, av, av_s)
    load_t = pltpu.make_async_copy(tapers, tv, tv_s)
    load_c = pltpu.make_async_copy(cells_hbm, cells, obs_s.at[0])
    load_v = pltpu.make_async_copy(values_hbm, values, obs_s.at[1])
    load_i = pltpu.make_async_copy(tab0_hbm, tab0, obs_s.at[2])
    for load in (load_c, load_v, load_i, load_a, load_t):
        load.start()

    def remote(src, dst, send, recv, target):
        return pltpu.make_async_remote_copy(
            src_ref=src, dst_ref=dst, send_sem=send, recv_sem=recv,
            device_id=target, device_id_type=MESH,
        )

    def members_of(c, shift):
        return pl.ds(pl.multiple_of(((c + shift * heavy) % chunks) * MC, MC), MC)

    def piece(ref, c, h, shift):
        return ref.at[pl.ds(h * half, half), members_of(c, shift), :]

    def send2(c, h):
        return remote(
            piece(anom, c, h, odd), piece(r2, c, h, 0), s2.at[c, h], q2.at[c, h], at(-2 * sign, 0)
        )

    def send1(c):
        return remote(
            anom.at[:, members_of(c, 1 - odd), :], r1.at[:, members_of(c, 0), :],
            s1.at[c], q1.at[c], at(sign, 0),
        )

    def to(u):
        return sign if u == 1 else -2 * sign

    def send_tab(u):
        return remote(tabs.at[u - 1], tab_in.at[u - 1], tab_s.at[u - 1], tab_r.at[u - 1], at(to(u), 0))

    def send_innov(u):
        return remote(innov, innov_in.at[u - 1], in_s.at[u - 1], in_r.at[u - 1], at(to(u), 0))

    def send_part(u, k):
        return remote(
            part.at[u, (me + k) % members], got.at[u, k], ps.at[u, k], pr.at[u, k],
            at((0, sign, 2 * sign)[u], k),
        )

    pl.semaphore_wait(barrier, len(greeted))
    for u in (1, 2):
        send_tab(u).start()
    for h in range(PIECES):
        send2(0, h).start()
    send1(0).start()
    acc[...] = jnp.zeros_like(acc)

    def hot_row(k, carry):
        cell = cells[pl.ds(k, 1), :]
        value = values[pl.ds(k, 1), :]
        lo = cell & (LANES - 1)
        block = cell // width
        group = (cell // LANES) % groups
        hi = group * blocks + block
        v1 = value.astype(jnp.bfloat16).astype(jnp.float32)
        rest = value - v1
        v2 = rest.astype(jnp.bfloat16).astype(jnp.float32)
        v3 = rest - v2
        rows = blocks * groups
        same = lax.broadcasted_iota(jnp.int32, (rows, LANES), 0) == hi
        where = pl.ds(pl.multiple_of(k * LANES, LANES), LANES)
        for n, v in enumerate((v1, v2, v3)):
            hot[pl.ds(n * rows, rows), where] = jnp.where(
                same, jnp.broadcast_to(v, (rows, LANES)), 0.0
            ).astype(jnp.bfloat16)
        low[:, where] = jnp.where(
            lax.broadcasted_iota(jnp.int32, (LANES, LANES), 0) == lo, 1.0, 0.0
        ).astype(jnp.bfloat16)
        return carry

    load_c.wait()
    load_v.wait()
    load_i.wait()
    lax.fori_loop(0, cells.shape[0], hot_row, 0)
    rows = blocks * groups
    sums = lax.dot_general(
        hot[...], low[...], (((1,), (1,)), ((), ())), preferred_element_type=jnp.float32
    )
    total = sums[0:rows] + sums[rows : 2 * rows] + sums[2 * rows : 3 * rows]
    for g in range(groups):
        innov[:, g * LANES : (g + 1) * LANES] = total[g * blocks : (g + 1) * blocks]
    for u in (1, 2):
        send_innov(u).start()

    def send_all(c, carry):
        for h in range(PIECES):
            send2(c, h).start()
        return carry

    for c in range(1, heavy):
        send1(c).start()
    lax.fori_loop(1, chunks, send_all, 0)
    for k in range(1, members):
        pl.semaphore_signal(peers, inc=1, device_id=at(0, k), device_id_type=MESH)

    load_a.wait()
    for c in range(chunks):
        for j in range(blocks):
            own_w[c, j] = (
                av[j, members_of(c, odd), :].astype(jnp.float32) * innov[pl.ds(j, 1), :]
            ).astype(jnp.bfloat16)
    load_t.wait()
    nw = width // 2

    def own_z(n, carry):
        t, x = n // 2, n % 2
        where = pl.ds(pl.multiple_of(x * nw, nw), nw)
        res = lax.dot_general(
            own_w[...].reshape(chunks * blocks * MC, width), tv[t, where, :],
            (((1,), (1,)), ((), ())), preferred_element_type=jnp.float32,
        )
        z[:, pl.ds(t * 3 * blocks, blocks), :, where] = res.reshape(chunks, blocks, MC, nw)
        return carry

    lax.fori_loop(0, KT * 2, own_z, 0)
    for c in range(heavy, chunks):
        for t in range(KT):
            z[c, (t * 3 + 1) * blocks : (t * 3 + 2) * blocks] = jnp.zeros((blocks, MC, width), jnp.float32)
    for c in range(chunks):
        z[c, zero_panel] = jnp.zeros((MC, width), jnp.float32)

    for u in (1, 2):
        send_tab(u).wait_recv()
        fill = pltpu.make_async_copy(tab_in.at[u - 1], idx.at[u - 1], idx_s.at[u - 1])
        fill.start()
        fill.wait()

    def pairs(c, u, table, source, shift):
        def one(i, carry):
            total = z[c, table(i, 0)]
            for s in range(1, slots):
                total = total + z[c, table(i, s)]
            value = source[i, members_of(c, shift), :].astype(jnp.float32) * total
            acc[u, i] += jnp.sum(value.reshape(MC // 8, 8, width), axis=0)
            return carry

        lax.fori_loop(0, blocks, one, 0)

    def fold(u):
        for i in range(blocks):
            row = jnp.sum(acc[u, i], axis=0, keepdims=True)
            for m in range(members):
                part[u, m, i : i + 1, :] = row[:, m * cols : (m + 1) * cols]

    def step(full, c, carry):
        for h in range(PIECES):
            send2(c, h).wait_recv()
        if full:
            send1(c).wait_recv()
        else:
            pairs(c, 2, lambda i, s: idx[1, i, s], r2, 0)

            @pl.when(c == chunks - 1)
            def _():
                fold(2)
                for k in range(members):
                    send_part(2, k).start()

        first = 0 if full else blocks
        for g, r in enumerate((r1, r2)):
            if g or full:
                for j in range(blocks):
                    wr[g * blocks + j] = (
                        r[j, members_of(c, 0), :].astype(jnp.float32)
                        * innov_in[g, pl.ds(j, 1), :]
                    ).astype(jnp.bfloat16)
        count = 2 * blocks - first

        def far_z(n, carry):
            t, x = n // 2, n % 2
            where = pl.ds(pl.multiple_of(x * nw, nw), nw)
            res = lax.dot_general(
                wr[pl.ds(first, count)].reshape(count * MC, width), tv[t, where, :],
                (((1,), (1,)), ((), ())), preferred_element_type=jnp.float32,
            )
            z[c, pl.ds(t * 3 * blocks + blocks + first, count), :, where] = res.reshape(
                count, MC, nw
            )
            return carry

        lax.fori_loop(0, KT * 2, far_z, 0)
        if full:
            pairs(c, 2, lambda i, s: idx[1, i, s], r2, 0)
            pairs(c, 1, lambda i, s: idx[0, i, s], r1, 0)
        pairs(c, 0, lambda i, s: tab0[i, s], av, odd)
        return carry

    for u in (1, 2):
        send_innov(u).wait_recv()
    lax.fori_loop(0, heavy, functools.partial(step, True), 0)
    fold(1)
    pl.semaphore_wait(peers, members - 1)
    for k in range(members):
        send_part(1, k).start()
    lax.fori_loop(heavy, chunks, functools.partial(step, False), 0)
    fold(0)
    for k in range(1, members):
        send_part(0, k).start()
    total = part[0, me]
    for u in (2, 1, 0):
        for k in range(members):
            if u or k:
                send_part(u, k).wait_recv()
                total = total + got[u, k]
    out[...] = total / jnp.float32(M - 1)

    for u in (0, 1, 2):
        for k in range(members):
            if u or k:
                send_part(u, k).wait_send()
    for u in (1, 2):
        send_tab(u).wait_send()
        send_innov(u).wait_send()

    def drain(c, carry):
        for h in range(PIECES):
            send2(c, h).wait_send()
        return carry

    lax.fori_loop(0, chunks, drain, 0)
    for c in range(heavy):
        send1(c).wait_send()


def on_device(states, members, anomalies, tapers, nbr_block, taper_index, pair_count, obs_cell, obs_value):
    blocks, mem, width = anomalies.shape
    slots = nbr_block.shape[1]
    chunks = mem // MC
    cols = width // members
    d = lax.axis_index("state")
    gap = (nbr_block // blocks - d + HOPS + states) % states - HOPS
    valid = jnp.arange(slots, dtype=jnp.int32)[None, :] < pair_count[:, None]
    base = taper_index * (3 * blocks) + nbr_block % blocks
    none = KT * 3 * blocks
    sign = 1 - 2 * (d % 2)
    gap = gap * sign
    tab0 = jnp.where(valid & (gap >= 0), base + gap * blocks, none)
    tab0 = jnp.pad(tab0, ((0, 0), (0, LANES - slots)))
    near = jnp.where(gap == 1, base, jnp.where(gap == -1, base + 2 * blocks, none))
    far = jnp.where(gap == -2, base, jnp.where(gap == -1, base + blocks, none))
    tabs = jnp.where(valid, jnp.stack([near, far]), none)
    tabs = jnp.pad(tabs, ((0, 0), (0, 0), (0, LANES - slots)))
    cells = obs_cell.reshape(-1, LANES)
    values = obs_value.reshape(-1, LANES)
    rows = blocks * (width // LANES)
    dma = pltpu.SemaphoreType.DMA
    any_space = pl.BlockSpec(memory_space=pl.ANY)
    vmem = pl.BlockSpec(memory_space=pltpu.VMEM)
    return pl.pallas_call(
        functools.partial(kernel, states, members, slots),
        out_shape=jax.ShapeDtypeStruct((blocks, cols), jnp.float32),
        in_specs=[any_space] * 6,
        out_specs=vmem,
        scratch_shapes=[
            pltpu.SMEM((blocks, LANES), jnp.int32),
            pltpu.VMEM(cells.shape, jnp.int32),
            pltpu.VMEM(values.shape, jnp.float32),
            dma((3,)),
            pltpu.VMEM((blocks, mem, width), jnp.bfloat16),
            pltpu.VMEM(tapers.shape, jnp.bfloat16),
            pltpu.VMEM((blocks, mem, width), jnp.bfloat16),
            pltpu.VMEM((blocks, mem, width), jnp.bfloat16),
            pltpu.VMEM((2, blocks, LANES), jnp.int32),
            pltpu.SMEM((2, blocks, LANES), jnp.int32),
            pltpu.VMEM((blocks, width), jnp.float32),
            pltpu.VMEM((2, blocks, width), jnp.float32),
            pltpu.VMEM((3 * rows, obs_cell.shape[0]), jnp.bfloat16),
            pltpu.VMEM((LANES, obs_cell.shape[0]), jnp.bfloat16),
            pltpu.VMEM((chunks, KT * 3 * blocks + 1, MC, width), jnp.float32),
            pltpu.VMEM((chunks, blocks, MC, width), jnp.bfloat16),
            pltpu.VMEM((2 * blocks, MC, width), jnp.bfloat16),
            pltpu.VMEM((3, blocks, 8, width), jnp.float32),
            pltpu.VMEM((3, members, blocks, cols), jnp.float32),
            pltpu.VMEM((3, members, blocks, cols), jnp.float32),
            dma((2,)), dma((2,)), dma((2,)), dma, dma,
            dma((chunks,)), dma((chunks,)),
            dma((chunks, PIECES)), dma((chunks, PIECES)),
            dma((2,)), dma((2,)),
            dma((3, members)), dma((3, members)),
            pltpu.SemaphoreType.REGULAR,
        ],
        compiler_params=pltpu.CompilerParams(
            collective_id=0, has_side_effects=True, vmem_limit_bytes=67_043_328
        ),
    )(tab0, tabs, cells, values, anomalies, tapers)


def solution(mesh):
    placed = (
        P("state", "member", None),
        P(),
        P("state", None),
        P("state", None),
        P("state"),
        P("state"),
        P("state"),
    )
    return jax.shard_map(
        functools.partial(on_device, mesh.shape["state"], mesh.shape["member"]),
        mesh=mesh, in_specs=placed, out_specs=P("state", "member"), check_vma=False,
    )
```
